32 devices in a mesh: groups: 2 (over x), cache: 8 (over z, y), mp: 2 (over core).
Axes of the slice: x: 2, y: 2, z: 4, core: 2. Of those that a mesh axis runs over, the one named last changes fastest.
Arguments:
- acceptance_signal: bfloat16 [512, 2048], P(('groups', 'cache'), 'mp'), parts along dimension 0, may hold values from -6 to 6
- address_vectors: bfloat16 [512, 2048], P(('groups', 'cache'), 'mp'), parts along dimension 0, may hold values from -0.75 to 0.75
- payload_vectors: bfloat16 [512, 2048], P(('groups', 'cache'), 'mp'), parts along dimension 0, may hold values from -6 to 6
- logarithmic_fading: bfloat16 [512, 2048], P(('groups', 'cache'), 'mp'), parts along dimension 0, may hold values from -10 to 0
- presigmoid_switch: bfloat16 [512, 2048], P(('groups', 'cache'), 'mp'), parts along dimension 0, may hold values from -6 to 6
- diagonal_reward_coefficients: float32 [2048], P('mp'), may hold values from -4 to 4
- layernorm_scaling: float32 [2048], P('mp'), may hold values from 0.5 to 1.5
- layernorm_shift: float32 [2048], P('mp'), may hold values from -1.5 to 1.5
- stored_memory_matrices: float32 [80, 32, 4096], P(('groups', 'cache'), 'mp'), parts along dimension 0, may hold values from -3 to 3
- holder_location: int32 [80], P('groups'), parts along dimension 0, may hold values from 0 to 39, as said below
- conversation_label: int32 [64], P(('groups', 'cache')), parts along dimension 0, may hold values from 0 to 39, as said below
- fresh_entry_amounts: int32 [64], P(('groups', 'cache')), parts along dimension 0, may hold values from 1 to 8, as said below
Outputs:
- time_mixed: bfloat16 [512, 2048], P(('groups', 'cache'), 'mp'), parts along dimension 0
- updated_store: float32 [80, 32, 4096], P(('groups', 'cache'), 'mp'), parts along dimension 0
The draws below stay inside these ranges and needn't reach their ends.
There are 2 independent parts, one for each index of `groups`. The reference program is written for one: setup_inputs(seed, part) draws one part's arguments, and reference() takes and returns one part's arrays. A program takes and returns all parts, laid end to end along the dimension named above; an argument that names none is the same for every part. Nothing has to cross between parts.
Inputs may be any that keep to these rules, and one draw needn't show every extreme that they name: A permutation: session s's state is row holder_location[s] of stored_memory_matrices, held by the owner holder_location[s] // 5. `conversation_label`: distinct sessions; the 4 sessions of one device lie with 4 distinct owners; one owner holds up to 5 served sessions, and in every draw some owner holds exactly 5. `fresh_entry_amounts`: in every draw some device's sessions all have 8 tokens.
All inputs are finite; a program needn't handle non-finite values.
Results may differ from the reference program's by a relative error of at most 0.001.
Values may be sent and summed in bfloat16 or wider, within the bound.
No kernel may reach another device: no remote copies, remote signals or barrier semaphores. Data moves between devices by JAX's collectives and lax.ppermute only.
A program may use at most 128 MiB of HBM per device.

```python
import jax
import jax.numpy as jnp
from jax import lax

GROUPS_HERE = 32
GROUP_WIDTH = 64
TOKEN_SLOTS = 8
SESS_DEV = 4
ALL_FEATURES = 2048
SESSION_TOTAL = 32
TOKENS = 256
STORED = 40


def routing_tables(key):
    random_subkeys = jax.random.split(key, 6)
    owner_total = SESSION_TOTAL // SESS_DEV
    per_owner = STORED // owner_total
    block_total = owner_total // SESS_DEV
    hot_count = min(per_owner, owner_total)
    owner_order = jax.random.permutation(random_subkeys[0], owner_total)
    device_order = jax.random.permutation(random_subkeys[1], owner_total)
    device_index = jnp.arange(owner_total, dtype=jnp.int32)
    position_of = jnp.zeros((owner_total,), jnp.int32).at[device_order].set(device_index)
    spill = jax.random.randint(random_subkeys[2], (owner_total,), 0, max(block_total - 1, 1)) + 1
    block_of = jnp.where(position_of < hot_count, 0, spill)
    rotation = jax.random.randint(random_subkeys[3], (owner_total, 1), 0, SESS_DEV)
    column = jnp.arange(SESS_DEV, dtype=jnp.int32)[None, :]
    owner_of = owner_order[block_of[:, None] * SESS_DEV + (column + rotation) % SESS_DEV]
    same_block = block_of[:, None] == block_of[None, :]
    before = device_index[None, :] < device_index[:, None]
    within = jnp.sum((same_block & before).astype(jnp.int32), axis=1)
    offset_draw = jax.random.randint(random_subkeys[4], (owner_total,), 0, per_owner)
    local_row = (within[:, None] + offset_draw[owner_of]) % per_owner
    slot_of = (owner_of * per_owner + local_row).reshape(SESSION_TOTAL)
    ranks = jax.random.permutation(random_subkeys[5], STORED).astype(jnp.int32) + 1
    ranks = ranks.at[slot_of[0]].set(0)
    ranks = ranks.at[slot_of[1]].set(STORED + 1)
    placement = jnp.argsort(ranks, stable=True).astype(jnp.int32)
    inverse = jnp.zeros((STORED,), jnp.int32).at[placement].set(jnp.arange(STORED, dtype=jnp.int32))
    session_list = inverse[slot_of]
    return (placement, session_list.astype(jnp.int32))


def draw_holder_location(key, part):
    placement, session_list = routing_tables(jax.random.fold_in(key, 11))
    return placement


def draw_conversation_label(key, part):
    placement, session_list = routing_tables(jax.random.fold_in(key, 11))
    return session_list


def draw_fresh_entry_amounts(key, part):
    random_subkeys = jax.random.split(jax.random.fold_in(key, 23), 3)
    device_total = SESSION_TOTAL // SESS_DEV
    counts = jax.random.randint(random_subkeys[0], (SESSION_TOTAL,), 1, TOKEN_SLOTS + 1)
    full_device = jax.random.randint(random_subkeys[1], (), 0, device_total)
    session_index = jnp.arange(SESSION_TOTAL, dtype=jnp.int32)
    counts = jnp.where(session_index // SESS_DEV == full_device, TOKEN_SLOTS, counts)
    short_at = (full_device + 1) % device_total * SESS_DEV + jax.random.randint(random_subkeys[2], (), 0, SESS_DEV)
    counts = jnp.where(session_index == short_at, 1, counts)
    return counts.astype(jnp.int32)


def draw_logarithmic_fading(key, part):
    random_subkeys = jax.random.split(jax.random.fold_in(key, 37), 5)
    base_rate = jnp.exp(jax.random.uniform(random_subkeys[0], (1, 1, ALL_FEATURES), jnp.float32, jnp.log(1.0 / 1000.0), jnp.log(1.0 / 8.0)))
    session_factor = jnp.exp(jax.random.uniform(random_subkeys[1], (SESSION_TOTAL, 1, 1), jnp.float32, jnp.log(0.5), jnp.log(2.0)))
    jitter = jnp.exp(jax.random.uniform(random_subkeys[2], (SESSION_TOTAL, TOKEN_SLOTS, ALL_FEATURES), jnp.float32, jnp.log(0.7), jnp.log(1.4)))
    decay_factor = base_rate * session_factor * jitter
    spike_mask = jax.random.randint(random_subkeys[3], (SESSION_TOTAL, TOKEN_SLOTS), 0, 12) == 0
    spike_rate = jnp.exp(jax.random.uniform(random_subkeys[4], (SESSION_TOTAL, TOKEN_SLOTS, 1), jnp.float32, jnp.log(0.22), jnp.log(0.69)))
    decay_factor = jnp.where(spike_mask[:, :, None], spike_rate, decay_factor)
    return jnp.log(decay_factor).reshape(TOKENS, ALL_FEATURES).astype(jnp.bfloat16)


def block_levels(own_key, shape, shards, smallest, largest):
    factor_of = 1.0
    for dim, parts in shards:
        draws = jax.random.uniform(jax.random.fold_in(jax.random.fold_in(own_key, 6), dim), (parts,), jnp.float32, smallest / len(shards), largest / len(shards))
        factor_of = factor_of * jnp.repeat(jnp.exp(draws), shape[dim] // parts).reshape((-1,) + (1,) * (len(shape) - 1 - dim))
    return factor_of


def normal_values(own_key, dims, width, bound, cuts=(), held_as=jnp.bfloat16):
    array = width * jax.random.normal(own_key, dims, jnp.float32)
    if cuts:
        array = array * block_levels(own_key, dims, cuts, -0.22, 0.18)
    return jnp.clip(array, -bound, bound).astype(held_as)


def setup_inputs(seed: int = 0, part: int = 0) -> dict:
    key_list = jax.random.split(jax.random.key(seed), 13)
    part_keys = jax.random.split(jax.random.fold_in(key_list[12], part), 13)
    return {
        "acceptance_signal": normal_values(part_keys[0], (TOKENS, ALL_FEATURES), 1.0, 6.0, ((0, 8), (1, 2))),
        "address_vectors": normal_values(part_keys[1], (TOKENS, ALL_FEATURES), 0.125, 0.75, ((0, 8), (1, 2))),
        "payload_vectors": normal_values(part_keys[2], (TOKENS, ALL_FEATURES), 1.0, 6.0, ((0, 8), (1, 2))),
        "logarithmic_fading": draw_logarithmic_fading(jax.random.fold_in(jax.random.fold_in(key_list[12], part), 71), part),
        "presigmoid_switch": normal_values(part_keys[4], (TOKENS, ALL_FEATURES), 1.0, 6.0, ((0, 8), (1, 2))),
        "diagonal_reward_coefficients": normal_values(key_list[5], (ALL_FEATURES,), 1.0, 4.0, ((0, 2),), jnp.float32),
        "layernorm_scaling": jnp.clip(1.0 + 0.1 * jax.random.normal(key_list[6], (ALL_FEATURES,), jnp.float32), 0.5, 1.5),
        "layernorm_shift": normal_values(key_list[7], (ALL_FEATURES,), 0.3, 1.5, ((0, 2),), jnp.float32),
        "stored_memory_matrices": normal_values(part_keys[8], (STORED, GROUPS_HERE, GROUP_WIDTH * GROUP_WIDTH), 0.5, 3.0, ((0, 8), (1, 2)), jnp.float32),
        "holder_location": draw_holder_location(jax.random.fold_in(jax.random.fold_in(key_list[12], part), 71), part),
        "conversation_label": draw_conversation_label(jax.random.fold_in(jax.random.fold_in(key_list[12], part), 71), part),
        "fresh_entry_amounts": draw_fresh_entry_amounts(jax.random.fold_in(jax.random.fold_in(key_list[12], part), 71), part),
    }


EPS = 0.00064

def reference(acceptance_signal, address_vectors, payload_vectors, logarithmic_fading, presigmoid_switch, diagonal_reward_coefficients, layernorm_scaling, layernorm_shift, stored_memory_matrices, holder_location, conversation_label, fresh_entry_amounts):
    slot_rows = holder_location[conversation_label]
    start_state = stored_memory_matrices[slot_rows].reshape(SESSION_TOTAL, GROUPS_HERE, GROUP_WIDTH, GROUP_WIDTH)

    def heads_view(tensor):
        return tensor.astype(jnp.float32).reshape(SESSION_TOTAL, TOKEN_SLOTS, GROUPS_HERE, GROUP_WIDTH).transpose(1, 0, 2, 3)
    acceptance_vectors = heads_view(acceptance_signal)
    address_by_group = heads_view(address_vectors)
    value_heads = heads_view(payload_vectors)
    decay_rate = jnp.exp(-jnp.exp(heads_view(logarithmic_fading)))
    diagonal_reward_array = diagonal_reward_coefficients.reshape(GROUPS_HERE, GROUP_WIDTH)

    def advance(evolving_memory, inputs):
        current_acceptance, step_k, step_v, step_w, position = inputs
        dyadic_contribution = step_k[..., :, None] * step_v[..., None, :]
        blended_result = lax.optimization_barrier(jnp.sum(current_acceptance[..., :, None] * (evolving_memory + diagonal_reward_array[None, :, :, None] * dyadic_contribution), axis=2))
        moved = step_w[..., :, None] * evolving_memory + dyadic_contribution
        valid_rows = (position < fresh_entry_amounts)[:, None, None, None]
        return (jnp.where(valid_rows, moved, evolving_memory), blended_result)
    positions = jnp.arange(TOKEN_SLOTS, dtype=jnp.int32)
    final_state, outputs = lax.scan(advance, start_state, (acceptance_vectors, address_by_group, value_heads, decay_rate, positions))
    wkv = outputs.transpose(1, 0, 2, 3)
    centred = wkv - lax.optimization_barrier(jnp.mean(wkv, axis=3, keepdims=True))
    variance = lax.optimization_barrier(jnp.mean(centred * centred, axis=3, keepdims=True))
    normed = centred * lax.rsqrt(variance + EPS) * layernorm_scaling.reshape(GROUPS_HERE, GROUP_WIDTH) + layernorm_shift.reshape(GROUPS_HERE, GROUP_WIDTH)
    gate_rows = presigmoid_switch.astype(jnp.float32).reshape(SESSION_TOTAL, TOKEN_SLOTS, ALL_FEATURES)
    gated_rows = normed.reshape(SESSION_TOTAL, TOKEN_SLOTS, ALL_FEATURES) * jax.nn.silu(gate_rows)
    valid_tokens = positions[None, :] < fresh_entry_amounts[:, None]
    time_mixed = jnp.where(valid_tokens[:, :, None], gated_rows, 0.0).astype(jnp.bfloat16).reshape(TOKENS, ALL_FEATURES)
    updated_store = stored_memory_matrices.at[slot_rows].set(final_state.reshape(SESSION_TOTAL, GROUPS_HERE, GROUP_WIDTH * GROUP_WIDTH))
    return (time_mixed, updated_store)
```

```python
import functools

import jax
import jax.numpy as jnp
from jax import lax
from jax.experimental import pallas as pl
from jax.experimental.pallas import tpu as pltpu
from jax.sharding import PartitionSpec as P

GROUP_WIDTH = 64
EPS = 0.00064
LANES = 128
META = 128
F32 = jnp.float32
BF16 = jnp.bfloat16

SMEM = functools.partial(pl.BlockSpec, memory_space=pltpu.SMEM)
VMEM = functools.partial(pl.BlockSpec, memory_space=pltpu.VMEM)


def lane_ids(rows):
    return lax.broadcasted_iota(jnp.int32, (rows, LANES), 1)


def row_ids(rows):
    return lax.broadcasted_iota(jnp.int32, (rows, LANES), 0)


def place_of(hold, label, j, store_rows):
    location = hold[label[j]]
    owner = lax.div(location, jnp.int32(store_rows))
    return owner, location - owner * store_rows


def running_decay(w_tile):
    step = -jnp.exp(w_tile.astype(F32))
    rows = row_ids(step.shape[0])
    total = step
    shift = 1
    while shift < step.shape[0]:
        total = total + jnp.where(rows >= shift, pltpu.roll(total, shift, 0), 0.0)
        shift *= 2
    return step, total


def half_sums(x, low):
    first = jnp.sum(jnp.where(low, x, 0.0), axis=1, keepdims=True)
    second = jnp.sum(jnp.where(low, 0.0, x), axis=1, keepdims=True)
    return jnp.where(low, first, second)


def pack_kernel(store_rows, hold, label, count, r, k, v, w, out):
    devices, length, _ = out.shape
    channels = r.shape[1]
    lanes = lane_ids(length)
    for d in range(devices):
        out[d, :, 4 * channels :] = jnp.zeros((length, META), BF16)
    for j in range(label.shape[0]):
        owner, local = place_of(hold, label, j, store_rows)
        rows = pl.ds(j * length, length)
        for index, ref in enumerate((r, k, v, w)):
            out[owner, :, index * channels : (index + 1) * channels] = ref[rows, :]
        meta = jnp.where(lanes == 0, local + 1, jnp.where(lanes == 1, count[j], 0))
        out[owner, :, 4 * channels :] = meta.astype(F32).astype(BF16)


def meta_of(recv, source, base):
    tile = recv[source, :, base:].astype(F32)
    lanes = lane_ids(tile.shape[0])
    row = jnp.max(jnp.where(lanes == 0, tile, 0.0)).astype(jnp.int32) - 1
    return row, jnp.max(jnp.where(lanes == 1, tile, 0.0)).astype(jnp.int32)


def spread(scratch, column, tile, low, both):
    length = tile.shape[0]
    turned = pltpu.roll(tile, GROUP_WIDTH, 1)
    even = jnp.where(low, tile, turned) if both else tile
    odd = jnp.where(low, turned, tile) if both else turned
    scratch[pl.ds(2 * column * length, length), :] = even
    scratch[pl.ds((2 * column + 1) * length, length), :] = odd


def token_rows(length, group, t):
    return pl.ds(group * 8 * length + t, 8, stride=length)


def take(x, index):
    return jnp.take_along_axis(x, index, axis=1, mode="promise_in_bounds")


def state_read_kernel(recv, store, out, scratch, result):
    devices, length, channels = out.shape
    columns = channels // LANES
    groups = store.shape[1] // 8
    tiles = store.shape[2] // LANES
    low = lane_ids(length) < GROUP_WIDTH
    low8 = lane_ids(8) < GROUP_WIDTH
    half = jnp.where(low8, 0, 1)

    @pl.loop(0, devices)
    def _(source):
        row, _ = meta_of(recv, source, 4 * channels)

        @pl.when(row >= 0)
        def _():
            for c in range(columns):
                at = c * LANES
                step, total = running_decay(recv[source, :, 3 * channels + at : 3 * channels + at + LANES])
                decayed = recv[source, :, at : at + LANES].astype(F32) * jnp.exp(total - step)
                spread(scratch, c, decayed, low, False)
            for g in range(groups):
                queries = [scratch[token_rows(length, g, t), :] for t in range(length)]
                sums = [jnp.zeros((8, LANES), F32) for _ in range(length)]
                for tile in range(tiles):
                    state = store[row, g * 8 : g * 8 + 8, tile * LANES : (tile + 1) * LANES]
                    index = half + 2 * tile
                    for t in range(length):
                        sums[t] = sums[t] + take(queries[t], index) * state
                for t in range(length):
                    result[token_rows(length, g, t), :] = sums[t] + pltpu.roll(sums[t], GROUP_WIDTH, 1)
            for c in range(columns):
                even = result[2 * c * length : (2 * c + 1) * length, :]
                odd = result[(2 * c + 1) * length : (2 * c + 2) * length, :]
                out[source, :, c * LANES : (c + 1) * LANES] = jnp.where(low, even, odd)


def state_write_kernel(recv, after, store, out, keys, values, decays):
    del after
    devices, length, width = recv.shape
    channels = (width - META) // 4
    columns = channels // LANES
    groups = store.shape[1] // 8
    tiles = store.shape[2] // LANES
    low = lane_ids(length) < GROUP_WIDTH
    rows = row_ids(length)
    half = jnp.where(lane_ids(8) < GROUP_WIDTH, 0, 1)
    out[...] = store[...]

    @pl.loop(0, devices)
    def _(source):
        row, count = meta_of(recv, source, 4 * channels)

        @pl.when(row >= 0)
        def _():
            for c in range(columns):
                at = c * LANES
                _, total = running_decay(recv[source, :, 3 * channels + at : 3 * channels + at + LANES])
                last = jnp.sum(jnp.where(rows == count - 1, total, 0.0), axis=0, keepdims=True)
                gap = jnp.exp(jnp.minimum(last - total, 0.0))
                key = recv[source, :, channels + at : channels + at + LANES].astype(F32)
                value = recv[source, :, 2 * channels + at : 2 * channels + at + LANES].astype(F32)
                spread(keys, c, jnp.where(rows < count, key * gap, 0.0), low, False)
                spread(values, c, value, low, True)
                spread(decays, c, jnp.broadcast_to(jnp.exp(last), (length, LANES)), low, False)
            for g in range(groups):
                key_of = [keys[token_rows(length, g, t), :] for t in range(length)]
                value_of = [values[token_rows(length, g, t), :] for t in range(length)]
                decay = decays[token_rows(length, g, 0), :]
                for tile in range(tiles):
                    at = slice(tile * LANES, (tile + 1) * LANES)
                    index = half + 2 * tile
                    state = take(decay, index) * store[row, g * 8 : g * 8 + 8, at]
                    for t in range(length):
                        state = state + take(key_of[t], index) * value_of[t]
                    out[row, g * 8 : g * 8 + 8, at] = state


def local_kernel(r, k, v, w, bonus, after, out):
    del after
    length = 8
    sessions = r.shape[0] // length
    columns = r.shape[1] // LANES
    low = lane_ids(length) < GROUP_WIDTH
    rows = row_ids(length)

    @pl.loop(0, sessions)
    def _(j):
        at = pl.ds(pl.multiple_of(j * length, length), length)
        for c in range(columns):
            cols = slice(c * LANES, (c + 1) * LANES)
            step, total = running_decay(w[at, cols])
            query = r[at, cols].astype(F32)
            key = k[at, cols].astype(F32)
            value = v[at, cols].astype(F32)
            wkv = half_sums(query * bonus[:, cols] * key, low) * value
            decayed = query * jnp.exp(total - step)
            grown = key * jnp.exp(-total)
            for back in range(1, length):
                score = half_sums(decayed * pltpu.roll(grown, back, 0), low)
                wkv = wkv + jnp.where(rows >= back, score * pltpu.roll(value, back, 0), 0.0)
            out[at, cols] = wkv


def finish_kernel(store_rows, hold, label, count, recv, part, gate, gain, shift, out):
    _, length, channels = recv.shape
    low = lane_ids(length) < GROUP_WIDTH
    rows = row_ids(length)
    for j in range(label.shape[0]):
        owner, _ = place_of(hold, label, j, store_rows)
        at = slice(j * length, (j + 1) * length)
        for c in range(channels // LANES):
            cols = slice(c * LANES, (c + 1) * LANES)
            wkv = recv[owner, :, cols] + part[at, cols]
            centred = wkv - half_sums(wkv, low) * (1.0 / GROUP_WIDTH)
            variance = half_sums(centred * centred, low) * (1.0 / GROUP_WIDTH)
            normed = centred * lax.rsqrt(variance + EPS) * gain[:, cols] + shift[:, cols]
            g = gate[at, cols].astype(F32)
            gated = normed * (g / (1.0 + jnp.exp(-g)))
            out[at, cols] = jnp.where(rows < count[j], gated, 0.0).astype(BF16)


def cost(flops, nbytes):
    return pl.CostEstimate(flops=flops, bytes_accessed=nbytes, transcendentals=0)


def shards(r, k, v, w, gate, bonus, gain, shift, store, hold, label, count):
    devices = lax.axis_size("cache")
    sessions = label.shape[0]
    store_rows, heads, state = store.shape
    tokens, channels = r.shape
    length = tokens // sessions
    width = 4 * channels + META
    send = pl.pallas_call(
        functools.partial(pack_kernel, store_rows),
        out_shape=jax.ShapeDtypeStruct((devices, length, width), BF16),
        in_specs=[SMEM()] * 3 + [VMEM()] * 4,
        out_specs=VMEM(),
        name="pack",
    )(hold, label, count, r, k, v, w)
    recv = lax.all_to_all(send, "cache", split_axis=0, concat_axis=0, tiled=True)
    part = pl.pallas_call(
        local_kernel,
        out_shape=jax.ShapeDtypeStruct((tokens, channels), F32),
        in_specs=[VMEM()] * 5 + [pl.BlockSpec(memory_space=pl.ANY)],
        out_specs=VMEM(),
        cost_estimate=cost(8_000_000, 400_000),
        name="local",
    )(r, k, v, w, bonus.reshape(1, channels), send)
    back = pl.pallas_call(
        state_read_kernel,
        out_shape=jax.ShapeDtypeStruct((devices, length, channels), F32),
        in_specs=[VMEM()] * 2,
        out_specs=VMEM(),
        scratch_shapes=[pltpu.VMEM((heads * length, LANES), F32)] * 2,
        name="state_read",
    )(recv, store)
    returned = lax.all_to_all(back, "cache", split_axis=0, concat_axis=0, tiled=True)
    updated = pl.pallas_call(
        state_write_kernel,
        out_shape=jax.ShapeDtypeStruct(store.shape, F32),
        in_specs=[VMEM(), pl.BlockSpec(memory_space=pl.ANY), VMEM()],
        out_specs=VMEM(),
        scratch_shapes=[pltpu.VMEM((heads * length, LANES), F32)] * 3,
        cost_estimate=cost(8_000_000, 3_000_000),
        name="state_write",
    )(recv, back, store)
    mixed = pl.pallas_call(
        functools.partial(finish_kernel, store_rows),
        out_shape=jax.ShapeDtypeStruct((tokens, channels), BF16),
        in_specs=[SMEM()] * 3 + [VMEM()] * 5,
        out_specs=VMEM(),
        name="finish",
    )(hold, label, count, returned, part, gate, gain.reshape(1, channels), shift.reshape(1, channels))
    return mixed, updated


def solution(mesh):
    rows = P(("groups", "cache"), "mp")
    states = P(("groups", "cache"), "mp", None)
    owned = P(("groups", "cache"))
    in_specs = (rows,) * 5 + (P("mp"),) * 3 + (states, P("groups"), owned, owned)
    return jax.shard_map(
        shards, mesh=mesh, in_specs=in_specs, out_specs=(rows, states), check_vma=False
    )
```

```python
import functools

import jax
import jax.numpy as jnp
from jax import lax
from jax.experimental import pallas as pl
from jax.experimental.pallas import tpu as pltpu
from jax.sharding import PartitionSpec as P

GROUP_WIDTH = 64
EPS = 0.00064
LANES = 128
META = 128
UNROLL = 4
F32 = jnp.float32
BF16 = jnp.bfloat16

SMEM = functools.partial(pl.BlockSpec, memory_space=pltpu.SMEM)
VMEM = functools.partial(pl.BlockSpec, memory_space=pltpu.VMEM)


def lane_ids(rows):
    return lax.broadcasted_iota(jnp.int32, (rows, LANES), 1)


def row_ids(rows):
    return lax.broadcasted_iota(jnp.int32, (rows, LANES), 0)


def place_of(hold, label, j, store_rows):
    location = hold[label[j]]
    owner = lax.div(location, jnp.int32(store_rows))
    return owner, location - owner * store_rows


def running_decay(w_tile):
    step = -jnp.exp(w_tile.astype(F32))
    rows = row_ids(step.shape[0])
    total = step
    shift = 1
    while shift < step.shape[0]:
        total = total + jnp.where(rows >= shift, pltpu.roll(total, shift, 0), 0.0)
        shift *= 2
    return step, total


def half_sums(x, low):
    first = jnp.sum(jnp.where(low, x, 0.0), axis=1, keepdims=True)
    second = jnp.sum(jnp.where(low, 0.0, x), axis=1, keepdims=True)
    return jnp.where(low, first, second)


def pack_kernel(store_rows, hold, label, count, r, k, v, w, out, route):
    devices, length, _ = out.shape
    channels = r.shape[1]
    lanes = lane_ids(length)
    for d in range(devices):
        out[d, :, 4 * channels :] = jnp.zeros((length, META), BF16)
    for j in range(label.shape[0]):
        owner, local = place_of(hold, label, j, store_rows)
        route[2 * j] = owner
        route[2 * j + 1] = count[j]
        rows = pl.ds(j * length, length)
        for index, ref in enumerate((r, k, v, w)):
            out[owner, :, index * channels : (index + 1) * channels] = ref[rows, :]
        meta = jnp.where(lanes == 0, local + 1, jnp.where(lanes == 1, count[j], 0))
        out[owner, :, 4 * channels :] = meta.astype(F32).astype(BF16)


def read_meta(recv, base, table):
    for source in range(recv.shape[0]):
        tile = recv[source, :, base:].astype(F32)
        lanes = lane_ids(tile.shape[0])
        tile = jnp.where(lanes == 0, 16.0 * tile, jnp.where(lanes == 1, tile, 0.0))
        first = jnp.sum(jnp.where(row_ids(tile.shape[0]) == 0, tile, 0.0))
        table[source] = first.astype(jnp.int32)


def spread(scratch, column, tile, low, both):
    length = tile.shape[0]
    turned = pltpu.roll(tile, GROUP_WIDTH, 1)
    even = jnp.where(low, tile, turned) if both else tile
    odd = jnp.where(low, turned, tile) if both else turned
    scratch[pl.ds(2 * column * length, length), :] = even
    scratch[pl.ds((2 * column + 1) * length, length), :] = odd


def token_rows(length, group, t):
    return pl.ds(group * 8 * length + t, 8, stride=length)


def take(x, index):
    return jnp.take_along_axis(x, index, axis=1, mode="promise_in_bounds")


def state_read_kernel(recv, store, part, out, table, scratch, result):
    del part
    devices, length, channels = out.shape
    columns = channels // LANES
    groups = store.shape[1] // 8
    tiles = store.shape[2] // LANES
    low = lane_ids(length) < GROUP_WIDTH
    half = jnp.where(lane_ids(8) < GROUP_WIDTH, 0, 1)
    read_meta(recv, 4 * channels, table)

    @pl.loop(0, devices)
    def _(source):
        row = lax.div(table[source], 16) - 1

        @pl.when(row >= 0)
        def _():
            for c in range(columns):
                at = c * LANES
                step, total = running_decay(recv[source, :, 3 * channels + at : 3 * channels + at + LANES])
                decayed = recv[source, :, at : at + LANES].astype(F32) * jnp.exp(total - step)
                spread(scratch, c, decayed, low, False)
            queries = [
                [scratch[token_rows(length, g, t), :] for t in range(length)] for g in range(groups)
            ]

            def accumulate(tile, sums):
                at = pl.ds(pl.multiple_of(tile * LANES, LANES), LANES)
                index = half + 2 * tile
                states = [store[row, g * 8 : g * 8 + 8, at] for g in range(groups)]
                return tuple(
                    tuple(sums[g][t] + take(queries[g][t], index) * states[g] for t in range(length))
                    for g in range(groups)
                )

            zero = jnp.zeros((8, LANES), F32)
            sums = lax.fori_loop(0, tiles, accumulate, ((zero,) * length,) * groups, unroll=UNROLL)
            for g in range(groups):
                for t in range(length):
                    total = sums[g][t]
                    result[token_rows(length, g, t), :] = total + pltpu.roll(total, GROUP_WIDTH, 1)
            for c in range(columns):
                even = result[2 * c * length : (2 * c + 1) * length, :]
                odd = result[(2 * c + 1) * length : (2 * c + 2) * length, :]
                out[source, :, c * LANES : (c + 1) * LANES] = jnp.where(low, even, odd)


def state_write_kernel(table, recv, after, store, out, keys, values, decays):
    del after
    devices, length, width = recv.shape
    channels = (width - META) // 4
    columns = channels // LANES
    groups = store.shape[1] // 8
    tiles = store.shape[2] // LANES
    low = lane_ids(length) < GROUP_WIDTH
    rows = row_ids(length)
    half = jnp.where(lane_ids(8) < GROUP_WIDTH, 0, 1)
    out[...] = store[...]

    @pl.loop(0, devices)
    def _(source):
        row = lax.div(table[source], 16) - 1
        count = lax.rem(table[source], 16)

        @pl.when(row >= 0)
        def _():
            for c in range(columns):
                at = c * LANES
                _, total = running_decay(recv[source, :, 3 * channels + at : 3 * channels + at + LANES])
                last = jnp.sum(jnp.where(rows == count - 1, total, 0.0), axis=0, keepdims=True)
                gap = jnp.exp(jnp.minimum(last - total, 0.0))
                key = recv[source, :, channels + at : channels + at + LANES].astype(F32)
                value = recv[source, :, 2 * channels + at : 2 * channels + at + LANES].astype(F32)
                spread(keys, c, jnp.where(rows < count, key * gap, 0.0), low, False)
                spread(values, c, value, low, True)
                spread(decays, c, jnp.broadcast_to(jnp.exp(last), (length, LANES)), low, False)
            span = range(length)
            key_of = [[keys[token_rows(length, g, t), :] for t in span] for g in range(groups)]
            value_of = [[values[token_rows(length, g, t), :] for t in span] for g in range(groups)]
            decay = [decays[token_rows(length, g, 0), :] for g in range(groups)]

            @pl.loop(0, tiles, unroll=UNROLL)
            def _(tile):
                at = pl.ds(pl.multiple_of(tile * LANES, LANES), LANES)
                index = half + 2 * tile
                for g in range(groups):
                    state = take(decay[g], index) * store[row, g * 8 : g * 8 + 8, at]
                    for t in span:
                        state = state + take(key_of[g][t], index) * value_of[g][t]
                    out[row, g * 8 : g * 8 + 8, at] = state


def local_kernel(r, k, v, w, bonus, after, out):
    del after
    length = 8
    sessions = r.shape[0] // length
    columns = r.shape[1] // LANES
    low = lane_ids(length) < GROUP_WIDTH
    rows = row_ids(length)

    @pl.loop(0, sessions)
    def _(j):
        at = pl.ds(pl.multiple_of(j * length, length), length)
        for c in range(columns):
            cols = slice(c * LANES, (c + 1) * LANES)
            step, total = running_decay(w[at, cols])
            query = r[at, cols].astype(F32)
            key = k[at, cols].astype(F32)
            value = v[at, cols].astype(F32)
            wkv = half_sums(query * bonus[:, cols] * key, low) * value
            decayed = query * jnp.exp(total - step)
            grown = key * jnp.exp(-total)
            for back in range(1, length):
                score = half_sums(decayed * pltpu.roll(grown, back, 0), low)
                wkv = wkv + jnp.where(rows >= back, score * pltpu.roll(value, back, 0), 0.0)
            out[at, cols] = wkv


def finish_kernel(route, recv, part, gate, gain, shift, out):
    _, length, channels = recv.shape
    low = lane_ids(length) < GROUP_WIDTH
    rows = row_ids(length)
    for j in range(out.shape[0] // length):
        owner, count = route[2 * j], route[2 * j + 1]
        at = slice(j * length, (j + 1) * length)
        for c in range(channels // LANES):
            cols = slice(c * LANES, (c + 1) * LANES)
            wkv = recv[owner, :, cols] + part[at, cols]
            centred = wkv - half_sums(wkv, low) * (1.0 / GROUP_WIDTH)
            variance = half_sums(centred * centred, low) * (1.0 / GROUP_WIDTH)
            normed = centred * lax.rsqrt(variance + EPS) * gain[:, cols] + shift[:, cols]
            g = gate[at, cols].astype(F32)
            gated = normed * (g / (1.0 + jnp.exp(-g)))
            out[at, cols] = jnp.where(rows < count, gated, 0.0).astype(BF16)


def cost(flops, nbytes):
    return pl.CostEstimate(flops=flops, bytes_accessed=nbytes, transcendentals=0)


PARAMS = pltpu.CompilerParams(vmem_limit_bytes=24 * 2**20)


def in_vmem(x):
    return pltpu.with_memory_space_constraint(x, pltpu.VMEM)


def in_smem(x):
    return pltpu.with_memory_space_constraint(x, pltpu.SMEM)


def shards(r, k, v, w, gate, bonus, gain, shift, store, hold, label, count):
    devices = lax.axis_size("cache")
    sessions = label.shape[0]
    store_rows, heads, state = store.shape
    tokens, channels = r.shape
    length = tokens // sessions
    width = 4 * channels + META
    send, route = pl.pallas_call(
        functools.partial(pack_kernel, store_rows),
        out_shape=(
            jax.ShapeDtypeStruct((devices, length, width), BF16),
            pltpu.SMEM((2 * sessions,), jnp.int32),
        ),
        in_specs=[SMEM()] * 3 + [VMEM()] * 4,
        out_specs=(VMEM(), SMEM()),
        compiler_params=PARAMS,
        name="pack",
    )(hold, label, count, r, k, v, w)
    recv = in_vmem(lax.all_to_all(send, "cache", split_axis=0, concat_axis=0, tiled=True))
    part = pl.pallas_call(
        local_kernel,
        out_shape=pltpu.VMEM((tokens, channels), F32),
        in_specs=[VMEM()] * 5 + [pl.BlockSpec(memory_space=pl.ANY)],
        out_specs=VMEM(),
        cost_estimate=cost(8_000_000, 400_000),
        compiler_params=PARAMS,
        name="local",
    )(r, k, v, w, bonus.reshape(1, channels), send)
    resident = in_vmem(store)
    back, table = pl.pallas_call(
        state_read_kernel,
        out_shape=(
            jax.ShapeDtypeStruct((devices, length, channels), F32),
            pltpu.SMEM((devices,), jnp.int32),
        ),
        in_specs=[VMEM()] * 3,
        out_specs=(VMEM(), SMEM()),
        scratch_shapes=[pltpu.VMEM((heads * length, LANES), F32)] * 2,
        compiler_params=PARAMS,
        name="state_read",
    )(recv, resident, in_vmem(part))
    returned = in_vmem(lax.all_to_all(back, "cache", split_axis=0, concat_axis=0, tiled=True))
    updated = pl.pallas_call(
        state_write_kernel,
        out_shape=jax.ShapeDtypeStruct(store.shape, F32),
        in_specs=[SMEM(), VMEM(), pl.BlockSpec(memory_space=pl.ANY), VMEM()],
        out_specs=VMEM(),
        scratch_shapes=[pltpu.VMEM((heads * length, LANES), F32)] * 3,
        cost_estimate=cost(8_000_000, 3_000_000),
        compiler_params=PARAMS,
        name="state_write",
    )(in_smem(table), recv, back, resident)
    mixed = pl.pallas_call(
        finish_kernel,
        out_shape=jax.ShapeDtypeStruct((tokens, channels), BF16),
        in_specs=[SMEM()] + [VMEM()] * 5,
        out_specs=VMEM(),
        compiler_params=PARAMS,
        name="finish",
    )(in_smem(route), returned, in_vmem(part), in_vmem(gate), gain.reshape(1, channels), shift.reshape(1, channels))
    return mixed, updated


def solution(mesh):
    rows = P(("groups", "cache"), "mp")
    states = P(("groups", "cache"), "mp", None)
    owned = P(("groups", "cache"))
    in_specs = (rows,) * 5 + (P("mp"),) * 3 + (states, P("groups"), owned, owned)
    return jax.shard_map(
        shards, mesh=mesh, in_specs=in_specs, out_specs=(rows, states), check_vma=False
    )
```

```python
import functools

import jax
import jax.numpy as jnp
from jax import lax
from jax.experimental import pallas as pl
from jax.experimental.pallas import tpu as pltpu
from jax.sharding import PartitionSpec as P

GROUP_WIDTH = 64
EPS = 0.00064
LANES = 128
META = 128
UNROLL = 4
F32 = jnp.float32
BF16 = jnp.bfloat16

SMEM = functools.partial(pl.BlockSpec, memory_space=pltpu.SMEM)
VMEM = functools.partial(pl.BlockSpec, memory_space=pltpu.VMEM)


def lane_ids(rows):
    return lax.broadcasted_iota(jnp.int32, (rows, LANES), 1)


def row_ids(rows):
    return lax.broadcasted_iota(jnp.int32, (rows, LANES), 0)


def place_of(hold, label, j, store_rows):
    location = hold[label[j]]
    owner = lax.div(location, jnp.int32(store_rows))
    return owner, location - owner * store_rows


def running_decay(w_tile):
    step = -jnp.exp(w_tile.astype(F32))
    rows = row_ids(step.shape[0])
    total = step
    shift = 1
    while shift < step.shape[0]:
        total = total + jnp.where(rows >= shift, pltpu.roll(total, shift, 0), 0.0)
        shift *= 2
    return step, total


def half_sums(x, low):
    first = jnp.sum(jnp.where(low, x, 0.0), axis=1, keepdims=True)
    second = jnp.sum(jnp.where(low, 0.0, x), axis=1, keepdims=True)
    return jnp.where(low, first, second)


def pack_kernel(store_rows, *refs):
    hold, label, count, *tensors = refs[:7]
    out, route, hold_in, label_in, count_in, meta, loaded, sems, sent = refs[7:]
    devices, length, _ = out.shape
    channels = tensors[0].shape[1]
    small = ((hold, hold_in), (label, label_in), (count, count_in))
    large = tuple((ref, loaded.at[index]) for index, ref in enumerate(tensors))
    loads = [
        pltpu.make_async_copy(source, target, sems.at[index])
        for index, (source, target) in enumerate(small + large)
    ]
    for load in loads:
        load.start()
    meta[...] = jnp.zeros(meta.shape, BF16)
    for load in loads[: len(small)]:
        load.wait()
    lanes = lane_ids(length)
    owners = []
    for j in range(label_in.shape[0]):
        owner, local = place_of(hold_in, label_in, j, store_rows)
        owners.append(owner)
        route[2 * j] = owner
        route[2 * j + 1] = count_in[j]
        tile = jnp.where(lanes == 0, local + 1, jnp.where(lanes == 1, count_in[j], 0))
        meta[owner] = tile.astype(F32).astype(BF16)
    sends = []
    for load in loads[len(small) :]:
        load.wait()
    for j, owner in enumerate(owners):
        for index in range(len(tensors)):
            sends.append(
                pltpu.make_async_copy(
                    loaded.at[index, j * length : (j + 1) * length],
                    out.at[owner, :, index * channels : (index + 1) * channels],
                    sent.at[len(sends)],
                )
            )
            sends[-1].start()
    sends.append(
        pltpu.make_async_copy(meta, out.at[:, :, len(tensors) * channels :], sent.at[len(sends)])
    )
    sends[-1].start()
    for send in sends:
        send.wait()


def read_meta(recv, base, table):
    for source in range(recv.shape[0]):
        tile = recv[source, :, base:].astype(F32)
        lanes = lane_ids(tile.shape[0])
        tile = jnp.where(lanes == 0, 16.0 * tile, jnp.where(lanes == 1, tile, 0.0))
        first = jnp.sum(jnp.where(row_ids(tile.shape[0]) == 0, tile, 0.0))
        table[source] = first.astype(jnp.int32)


def spread(scratch, column, tile, low, both):
    length = tile.shape[0]
    turned = pltpu.roll(tile, GROUP_WIDTH, 1)
    even = jnp.where(low, tile, turned) if both else tile
    odd = jnp.where(low, turned, tile) if both else turned
    scratch[pl.ds(2 * column * length, length), :] = even
    scratch[pl.ds((2 * column + 1) * length, length), :] = odd


def token_rows(length, group, t):
    return pl.ds(group * 8 * length + t, 8, stride=length)


def take(x, index):
    return jnp.take_along_axis(x, index, axis=1, mode="promise_in_bounds")


def split(x):
    high = x.astype(BF16)
    return high, (x - high.astype(F32)).astype(BF16)


def retile_kernel(store, part, out, scratch):
    del part
    tiles = store.shape[2] // LANES

    @pl.loop(0, store.shape[0])
    def _(row):
        for g in range(store.shape[1] // 8):
            for tile in range(tiles):
                scratch[g, tile * 8 : tile * 8 + 8, :] = store[
                    row, g * 8 : g * 8 + 8, tile * LANES : (tile + 1) * LANES
                ]
            for head in range(8):
                for tile in range(0, tiles, 16):
                    halves = [
                        scratch[g, pl.ds(head + 8 * (tile + more), 8, stride=8), :] for more in (0, 8)
                    ]
                    high, low = split(jnp.concatenate(halves, axis=0))
                    at = slice(head * tiles + tile, head * tiles + tile + 16)
                    out[row, g, at, :LANES] = high
                    out[row, g, at, LANES:] = low


def state_read_kernel(recv, matrices, out, table, order, queries):
    devices, length, channels = out.shape
    columns = channels // LANES
    _, groups, depth, _ = matrices.shape
    tiles = depth // 8
    per_group = columns // groups
    half_rows = 8 * 2 * length
    lanes = lane_ids(length)
    low = lanes < GROUP_WIDTH
    spot = lanes % tiles
    deal = (lanes // GROUP_WIDTH) * GROUP_WIDTH + 2 * spot + (lanes % GROUP_WIDTH) // tiles
    queries[...] = jnp.zeros(queries.shape, BF16)
    read_meta(recv, 4 * channels, table)

    served = jnp.int32(0)
    for source in range(devices):
        served = served + jnp.where(table[source] > 0, 1, 0)
    first, other = jnp.int32(0), served
    for source in range(devices):
        here = table[source] > 0
        order[jnp.where(here, first, other)] = jnp.int32(source)
        first = first + jnp.where(here, 1, 0)
        other = other + jnp.where(here, 0, 1)

    def lay_out(source):
        for c in range(columns):
            at = c * LANES
            step, total = running_decay(recv[source, :, 3 * channels + at : 3 * channels + at + LANES])
            decayed = recv[source, :, at : at + LANES].astype(F32) * jnp.exp(total - step)
            dealt = take(decayed, deal)
            for parity in range(2):
                head = 2 * (c % per_group) + parity
                quarter, side = head % 4, head // 4
                blocks = []
                for p in range(2):
                    shift = (quarter - (2 * parity + p)) * tiles % LANES
                    turned = pltpu.roll(dealt, shift, 1) if shift else dealt
                    blocks.append(jnp.where(lanes // tiles == quarter, turned, 0.0))
                high, rest = split(jnp.concatenate(blocks, axis=0))
                rows = head * 2 * length
                cols = slice(side * LANES, (side + 1) * LANES)
                queries[source, c // per_group, rows : rows + 2 * length, cols] = high
                queries[source, c // per_group, half_rows + rows : half_rows + rows + 2 * length, cols] = rest

    def read(index):
        source = order[index]
        row = jnp.maximum(lax.div(table[source], 16) - 1, 0)
        for g in range(groups):
            product = jnp.dot(queries[source, g], matrices[row, g], preferred_element_type=F32)
            product = product[:, :LANES] + product[:, LANES:]
            product = product[:half_rows] + product[half_rows:]
            for c in range(per_group):
                tile = [
                    product[(4 * c + part) * length : (4 * c + part + 1) * length] for part in range(4)
                ]
                even = tile[0] + pltpu.roll(tile[1], GROUP_WIDTH, 1)
                odd = pltpu.roll(tile[2], GROUP_WIDTH, 1) + tile[3]
                at = (g * per_group + c) * LANES
                out[source, :, at : at + LANES] = jnp.where(low, even, odd)

    loop(devices, lay_out)
    loop(min(devices, matrices.shape[0]), read)


def loop(trips, body):
    pl.loop(0, trips, unroll=trips if trips <= 8 else 1)(body)


def state_write_kernel(table, recv, after, store, out, keys, values, decays):
    del after
    devices, length, width = recv.shape
    channels = (width - META) // 4
    columns = channels // LANES
    groups = store.shape[1] // 8
    tiles = store.shape[2] // LANES
    low = lane_ids(length) < GROUP_WIDTH
    rows = row_ids(length)
    half = jnp.where(lane_ids(8) < GROUP_WIDTH, 0, 1)
    out[...] = store[...]

    @pl.loop(0, devices)
    def _(source):
        row = lax.div(table[source], 16) - 1
        count = lax.rem(table[source], 16)

        @pl.when(row >= 0)
        def _():
            for c in range(columns):
                at = c * LANES
                _, total = running_decay(recv[source, :, 3 * channels + at : 3 * channels + at + LANES])
                last = jnp.sum(jnp.where(rows == count - 1, total, 0.0), axis=0, keepdims=True)
                gap = jnp.exp(jnp.minimum(last - total, 0.0))
                key = recv[source, :, channels + at : channels + at + LANES].astype(F32)
                value = recv[source, :, 2 * channels + at : 2 * channels + at + LANES].astype(F32)
                spread(keys, c, jnp.where(rows < count, key * gap, 0.0), low, False)
                spread(values, c, value, low, True)
                spread(decays, c, jnp.broadcast_to(jnp.exp(last), (length, LANES)), low, False)
            span = range(length)
            key_of = [[keys[token_rows(length, g, t), :] for t in span] for g in range(groups)]
            value_of = [[values[token_rows(length, g, t), :] for t in span] for g in range(groups)]
            decay = [decays[token_rows(length, g, 0), :] for g in range(groups)]

            @pl.loop(0, tiles, unroll=UNROLL)
            def _(tile):
                at = pl.ds(pl.multiple_of(tile * LANES, LANES), LANES)
                index = half + 2 * tile
                for g in range(groups):
                    state = take(decay[g], index) * store[row, g * 8 : g * 8 + 8, at]
                    for t in span:
                        state = state + take(key_of[g][t], index) * value_of[g][t]
                    out[row, g * 8 : g * 8 + 8, at] = state


def local_kernel(r, k, v, w, bonus, after, out):
    del after
    length = 8
    sessions = r.shape[0] // length
    columns = r.shape[1] // LANES
    low = lane_ids(length) < GROUP_WIDTH
    rows = row_ids(length)

    @pl.loop(0, sessions)
    def _(j):
        at = pl.ds(pl.multiple_of(j * length, length), length)
        for c in range(columns):
            cols = slice(c * LANES, (c + 1) * LANES)
            step, total = running_decay(w[at, cols])
            query = r[at, cols].astype(F32)
            key = k[at, cols].astype(F32)
            value = v[at, cols].astype(F32)
            wkv = half_sums(query * bonus[:, cols] * key, low) * value
            decayed = query * jnp.exp(total - step)
            grown = key * jnp.exp(-total)
            for back in range(1, length):
                score = half_sums(decayed * pltpu.roll(grown, back, 0), low)
                wkv = wkv + jnp.where(rows >= back, score * pltpu.roll(value, back, 0), 0.0)
            out[at, cols] = wkv


def finish_kernel(route, recv, part, gate, gain, shift, out):
    _, length, channels = recv.shape
    low = lane_ids(length) < GROUP_WIDTH
    rows = row_ids(length)
    for j in range(out.shape[0] // length):
        owner, count = route[2 * j], route[2 * j + 1]
        at = slice(j * length, (j + 1) * length)
        for c in range(channels // LANES):
            cols = slice(c * LANES, (c + 1) * LANES)
            wkv = recv[owner, :, cols] + part[at, cols]
            centred = wkv - half_sums(wkv, low) * (1.0 / GROUP_WIDTH)
            variance = half_sums(centred * centred, low) * (1.0 / GROUP_WIDTH)
            normed = centred * lax.rsqrt(variance + EPS) * gain[:, cols] + shift[:, cols]
            g = gate[at, cols].astype(F32)
            gated = normed * (g / (1.0 + jnp.exp(-g)))
            out[at, cols] = jnp.where(rows < count, gated, 0.0).astype(BF16)


def cost(flops, nbytes):
    return pl.CostEstimate(flops=flops, bytes_accessed=nbytes, transcendentals=0)


PARAMS = pltpu.CompilerParams(vmem_limit_bytes=24 * 2**20)


def in_vmem(x):
    return pltpu.with_memory_space_constraint(x, pltpu.VMEM)


def in_hbm(x):
    return pltpu.with_memory_space_constraint(x, pltpu.HBM)


def in_smem(x):
    return pltpu.with_memory_space_constraint(x, pltpu.SMEM)


def shards(r, k, v, w, gate, bonus, gain, shift, store, hold, label, count):
    devices = lax.axis_size("cache")
    sessions = label.shape[0]
    store_rows, heads, state = store.shape
    tokens, channels = r.shape
    length = tokens // sessions
    width = 4 * channels + META
    anywhere = pl.BlockSpec(memory_space=pltpu.HBM)
    send, route = pl.pallas_call(
        functools.partial(pack_kernel, store_rows),
        out_shape=(
            jax.ShapeDtypeStruct((devices, length, width), BF16),
            pltpu.SMEM((2 * sessions,), jnp.int32),
        ),
        in_specs=[anywhere] * 7,
        out_specs=(anywhere, SMEM()),
        scratch_shapes=[
            pltpu.SMEM(hold.shape, jnp.int32),
            pltpu.SMEM(label.shape, jnp.int32),
            pltpu.SMEM(count.shape, jnp.int32),
            pltpu.VMEM((devices, length, META), BF16),
            pltpu.VMEM((4, tokens, channels), BF16),
            pltpu.SemaphoreType.DMA((7,)),
            pltpu.SemaphoreType.DMA((4 * sessions + 1,)),
        ],
        compiler_params=PARAMS,
        name="pack",
    )(*(in_hbm(x) for x in (hold, label, count, r, k, v, w)))
    recv = in_vmem(lax.all_to_all(send, "cache", split_axis=0, concat_axis=0, tiled=True))
    part = pl.pallas_call(
        local_kernel,
        out_shape=pltpu.VMEM((tokens, channels), F32),
        in_specs=[VMEM()] * 5 + [pl.BlockSpec(memory_space=pl.ANY)],
        out_specs=VMEM(),
        cost_estimate=cost(8_000_000, 400_000),
        compiler_params=PARAMS,
        name="local",
    )(r, k, v, w, bonus.reshape(1, channels), send)
    resident = in_vmem(store)
    groups, depth = heads // 8, 8 * state // LANES
    matrices = pl.pallas_call(
        retile_kernel,
        out_shape=pltpu.VMEM((store_rows, groups, depth, 2 * LANES), BF16),
        in_specs=[VMEM()] * 2,
        out_specs=VMEM(),
        scratch_shapes=[pltpu.VMEM((groups, depth, LANES), F32)],
        cost_estimate=cost(8_000_000, 2_000_000),
        compiler_params=PARAMS,
        name="retile",
    )(resident, in_vmem(part))
    back, table = pl.pallas_call(
        state_read_kernel,
        out_shape=(
            jax.ShapeDtypeStruct((devices, length, channels), F32),
            pltpu.SMEM((devices,), jnp.int32),
        ),
        in_specs=[VMEM()] * 2,
        out_specs=(VMEM(), SMEM()),
        scratch_shapes=[
            pltpu.SMEM((devices,), jnp.int32),
            pltpu.VMEM((devices, groups, 4 * 8 * length, depth), BF16),
        ],
        compiler_params=PARAMS,
        name="state_read",
    )(recv, in_vmem(matrices))
    returned = in_vmem(lax.all_to_all(back, "cache", split_axis=0, concat_axis=0, tiled=True))
    updated = pl.pallas_call(
        state_write_kernel,
        out_shape=jax.ShapeDtypeStruct(store.shape, F32),
        in_specs=[SMEM(), VMEM(), pl.BlockSpec(memory_space=pl.ANY), VMEM()],
        out_specs=VMEM(),
        scratch_shapes=[pltpu.VMEM((heads * length, LANES), F32)] * 3,
        cost_estimate=cost(8_000_000, 3_000_000),
        compiler_params=PARAMS,
        name="state_write",
    )(in_smem(table), recv, back, resident)
    mixed = pl.pallas_call(
        finish_kernel,
        out_shape=jax.ShapeDtypeStruct((tokens, channels), BF16),
        in_specs=[SMEM()] + [VMEM()] * 5,
        out_specs=VMEM(),
        compiler_params=PARAMS,
        name="finish",
    )(in_smem(route), returned, in_vmem(part), in_vmem(gate), gain.reshape(1, channels), shift.reshape(1, channels))
    return mixed, updated


def solution(mesh):
    rows = P(("groups", "cache"), "mp")
    states = P(("groups", "cache"), "mp", None)
    owned = P(("groups", "cache"))
    in_specs = (rows,) * 5 + (P("mp"),) * 3 + (states, P("groups"), owned, owned)
    return jax.shard_map(
        shards, mesh=mesh, in_specs=in_specs, out_specs=(rows, states), check_vma=False
    )
```

```python
import functools

import jax
import jax.numpy as jnp
from jax import lax
from jax.experimental import pallas as pl
from jax.experimental.pallas import tpu as pltpu
from jax.sharding import PartitionSpec as P

GROUP_WIDTH = 64
EPS = 0.00064
LANES = 128
META = 128
F32 = jnp.float32
BF16 = jnp.bfloat16

SMEM = functools.partial(pl.BlockSpec, memory_space=pltpu.SMEM)
VMEM = functools.partial(pl.BlockSpec, memory_space=pltpu.VMEM)


def lane_ids(rows):
    return lax.broadcasted_iota(jnp.int32, (rows, LANES), 1)


def row_ids(rows):
    return lax.broadcasted_iota(jnp.int32, (rows, LANES), 0)


def place_of(hold, label, j, store_rows):
    location = hold[label[j]]
    owner = lax.div(location, jnp.int32(store_rows))
    return owner, location - owner * store_rows


def running_decay(w_tile):
    step = -jnp.exp(w_tile.astype(F32))
    rows = row_ids(step.shape[0])
    total = step
    shift = 1
    while shift < step.shape[0]:
        total = total + jnp.where(rows >= shift, pltpu.roll(total, shift, 0), 0.0)
        shift *= 2
    return step, total


def half_sums(x, low):
    first = jnp.sum(jnp.where(low, x, 0.0), axis=1, keepdims=True)
    second = jnp.sum(jnp.where(low, 0.0, x), axis=1, keepdims=True)
    return jnp.where(low, first, second)


def pack_kernel(store_rows, *refs):
    me, hold, label, count, *tensors = refs[:8]
    out, late, route, hold_in, label_in, count_in, meta, loaded, sems, sent = refs[8:]
    devices, length, _ = out.shape
    channels = tensors[0].shape[1]
    small = ((hold, hold_in), (label, label_in), (count, count_in))
    large = tuple((ref, loaded.at[index]) for index, ref in enumerate(tensors))
    loads = [
        pltpu.make_async_copy(source, target, sems.at[index])
        for index, (source, target) in enumerate(small + large)
    ]
    for load in loads:
        load.start()
    meta[...] = jnp.zeros(meta.shape, BF16)
    for load in loads[: len(small)]:
        load.wait()
    lanes = lane_ids(length)
    owners = []
    for j in range(label_in.shape[0]):
        owner, local = place_of(hold_in, label_in, j, store_rows)
        owners.append(owner)
        route[2 * j] = owner
        route[2 * j + 1] = count_in[j]
        tile = jnp.where(lanes == 0, local + 1, jnp.where(lanes == 1, count_in[j], 0))
        meta[owner] = tile.astype(F32).astype(BF16)
    sends = []

    def ship(source, target):
        sends.append(pltpu.make_async_copy(source, target, sent.at[len(sends)]))
        sends[-1].start()

    for index in range(4):
        loads[len(small) + index].wait()
        for j, owner in enumerate(owners):
            block = loaded.at[index, j * length : (j + 1) * length]
            at = slice(index % 2 * channels, (index % 2 + 1) * channels)
            if index < 2:
                ship(block, out.at[owner, :, at])
            else:
                slot = jnp.bitwise_xor(owner, me[0])
                slot = lax.rem(slot, devices // 2) * 2 + lax.div(slot, devices // 2)
                ship(block, late.at[slot, :, at])
    ship(meta, out.at[:, :, 2 * channels :])
    for send in sends:
        send.wait()


def collect_kernel(after, slots, *refs):
    del after
    near, out, sems = refs[:-2], refs[-2], refs[-1]
    copies = [
        pltpu.make_async_copy(source.at[1], out.at[index], sems.at[index])
        for index, source in enumerate((slots, *near))
    ]
    for copy in copies:
        copy.start()
    for copy in copies:
        copy.wait()


def read_meta(recv, base, table):
    for source in range(recv.shape[0]):
        tile = recv[source, :, base:].astype(F32)
        lanes = lane_ids(tile.shape[0])
        tile = jnp.where(lanes == 0, 16.0 * tile, jnp.where(lanes == 1, tile, 0.0))
        first = jnp.sum(jnp.where(row_ids(tile.shape[0]) == 0, tile, 0.0))
        table[source] = first.astype(jnp.int32)


def spread(scratch, column, tile, low, both):
    length = tile.shape[0]
    turned = pltpu.roll(tile, GROUP_WIDTH, 1)
    even = jnp.where(low, tile, turned) if both else tile
    odd = jnp.where(low, turned, tile) if both else turned
    scratch[pl.ds(2 * column * length, length), :] = even
    scratch[pl.ds((2 * column + 1) * length, length), :] = odd


def token_rows(length, group, t):
    return pl.ds(group * 8 * length + t, 8, stride=length)


def take(x, index):
    return jnp.take_along_axis(x, index, axis=1, mode="promise_in_bounds")


def split(x):
    high = x.astype(BF16)
    return high, (x - high.astype(F32)).astype(BF16)


def retile_kernel(store, part, out, resident, scratch):
    del part
    tiles = store.shape[2] // LANES

    @pl.loop(0, store.shape[0])
    def _(row):
        for g in range(store.shape[1] // 8):
            for tile in range(tiles):
                at = slice(tile * LANES, (tile + 1) * LANES)
                block = store[row, g * 8 : g * 8 + 8, at]
                scratch[g, tile * 8 : tile * 8 + 8, :] = block
                resident[row, g * 8 : g * 8 + 8, at] = block
            for head in range(8):
                for tile in range(0, tiles, 16):
                    halves = [
                        scratch[g, pl.ds(head + 8 * (tile + more), 8, stride=8), :] for more in (0, 8)
                    ]
                    high, low = split(jnp.concatenate(halves, axis=0))
                    at = slice(head * tiles + tile, head * tiles + tile + 16)
                    out[row, g, at, :LANES] = high
                    out[row, g, at, LANES:] = low


def deal_lanes(lanes, tiles):
    return (
        (lanes // GROUP_WIDTH) * GROUP_WIDTH + 2 * (lanes % tiles) + (lanes % GROUP_WIDTH) // tiles
    )


def block_diagonal(tile, column, target, deal, lanes, tiles):
    length = tile.shape[0]
    half_rows = 8 * 2 * length
    dealt = take(tile, deal)
    for parity in range(2):
        head = 2 * column + parity
        quarter, side = head % 4, head // 4
        blocks = []
        for p in range(2):
            shift = (quarter - (2 * parity + p)) * tiles % LANES
            turned = pltpu.roll(dealt, shift, 1) if shift else dealt
            blocks.append(jnp.where(lanes // tiles == quarter, turned, 0.0))
        high, rest = split(jnp.concatenate(blocks, axis=0))
        rows = head * 2 * length
        cols = slice(side * LANES, (side + 1) * LANES)
        target[rows : rows + 2 * length, cols] = high
        target[half_rows + rows : half_rows + rows + 2 * length, cols] = rest


def loop(trips, body):
    pl.loop(0, trips, unroll=trips if trips <= 8 else 1)(body)


def state_read_kernel(recv, matrices, out, table, order, places, queries, ready, taken, sems):
    devices, length, channels = out.shape
    columns = channels // LANES
    store_rows, groups, depth, _ = matrices.shape
    tiles = depth // 8
    per_group = columns // groups
    half_rows = 8 * 2 * length
    lanes = lane_ids(length)
    low = lanes < GROUP_WIDTH
    deal = deal_lanes(lanes, tiles)
    queries[...] = jnp.zeros(queries.shape, BF16)
    read_meta(recv, 2 * channels, table)

    served = jnp.int32(0)
    for row in range(store_rows):
        taken[row] = 0
    for source in range(devices):
        served = served + jnp.where(table[source] > 0, 1, 0)
    first, other = jnp.int32(0), served
    for source in range(devices):
        here = table[source] > 0
        order[jnp.where(here, first, other)] = jnp.int32(source)
        row = jnp.maximum(lax.div(table[source], 16) - 1, 0)
        places[jnp.where(here, first, store_rows)] = row
        taken[row] = jnp.where(here, 1, taken[row])
        first = first + jnp.where(here, 1, 0)
        other = other + jnp.where(here, 0, 1)
    for row in range(store_rows):
        free = taken[row] == 0
        places[jnp.where(free, first, store_rows)] = jnp.int32(row)
        first = first + jnp.where(free, 1, 0)
    places[store_rows] = served

    def lay_out(source):
        for c in range(columns):
            at = c * LANES
            step, total = running_decay(recv[source, :, channels + at : channels + at + LANES])
            decayed = recv[source, :, at : at + LANES].astype(F32) * jnp.exp(total - step)
            target = queries.at[source, c // per_group]
            block_diagonal(decayed, c % per_group, target, deal, lanes, tiles)

    def read(index):
        source = order[index]
        row = jnp.maximum(lax.div(table[source], 16) - 1, 0)
        for g in range(groups):
            product = jnp.dot(queries[source, g], matrices[row, g], preferred_element_type=F32)
            product = product[:, :LANES] + product[:, LANES:]
            product = product[:half_rows] + product[half_rows:]
            for c in range(per_group):
                tile = [
                    product[(4 * c + part) * length : (4 * c + part + 1) * length] for part in range(4)
                ]
                even = tile[0] + pltpu.roll(tile[1], GROUP_WIDTH, 1)
                odd = pltpu.roll(tile[2], GROUP_WIDTH, 1) + tile[3]
                at = (g * per_group + c) * LANES
                ready[index, :, at : at + LANES] = jnp.where(low, even, odd)
        block(index).start()

    def block(index):
        return pltpu.make_async_copy(ready.at[index], out.at[order[index]], sems.at[index])

    loop(devices, lay_out)
    loop(ready.shape[0], read)
    loop(ready.shape[0], lambda index: block(index).wait())


def scale_kernel(table, order, places, recv, store, after, out, gaps, decays):
    del after
    _, length, width = recv.shape
    channels = (width - META) // 2
    columns = channels // LANES
    store_rows, heads, _ = store.shape
    groups = heads // 8
    tiles = store.shape[2] // LANES
    low = lane_ids(length) < GROUP_WIDTH
    rows = row_ids(length)
    half = jnp.where(lane_ids(8) < GROUP_WIDTH, 0, 1)

    def scale(index):
        row = places[index]

        @pl.when(index < places[store_rows])
        def _():
            source = order[index]
            count = lax.rem(table[source], 16)
            for c in range(columns):
                at = c * LANES
                _, total = running_decay(recv[source, :, channels + at : channels + at + LANES])
                last = jnp.sum(jnp.where(rows == count - 1, total, 0.0), axis=0, keepdims=True)
                gap = jnp.exp(jnp.minimum(last - total, 0.0))
                gaps[source, :, at : at + LANES] = jnp.where(rows < count, gap, 0.0)
                spread(decays, c, jnp.broadcast_to(jnp.exp(last), (length, LANES)), low, False)
            for g in range(groups):
                decay = decays[token_rows(length, g, 0), :]
                for tile in range(tiles):
                    at = slice(tile * LANES, (tile + 1) * LANES)
                    out[row, g * 8 : g * 8 + 8, at] = (
                        take(decay, half + 2 * tile) * store[row, g * 8 : g * 8 + 8, at]
                    )

        @pl.when(index >= places[store_rows])
        def _():
            out[row] = store[row]

    pl.loop(0, store_rows)(scale)


def state_write_kernel(where, order, places, me, gaps, scaled, *refs):
    late, (out, keys, values, turned, result, sems) = refs[:-6], refs[-6:]
    devices, length, channels = gaps.shape
    columns = channels // LANES
    store_rows, heads, _ = scaled.shape
    groups = heads // 8
    tiles = scaled.shape[2] // LANES
    per_group = columns // groups
    half_rows = 8 * 2 * length
    lanes = lane_ids(length)
    low = lanes < GROUP_WIDTH
    deal = deal_lanes(lanes, tiles)
    keys[...] = jnp.zeros(keys.shape, BF16)

    for slot, (array, block) in enumerate(where):
        source = jnp.bitwise_xor(jnp.int32(slot), me[0])
        for c in range(columns):
            at = c * LANES
            column = c % per_group
            key = late[array][block, :, at : at + LANES].astype(F32) * gaps[source, :, at : at + LANES]
            block_diagonal(key, column, keys.at[slot, c // per_group], deal, lanes, tiles)
            value = late[array][block, :, channels + at : channels + at + LANES].astype(F32)
            other = pltpu.roll(value, GROUP_WIDTH, 1)
            for parity, (near, far) in enumerate(((value, other), (other, value))):
                pair = jnp.concatenate((jnp.where(low, near, 0.0), jnp.where(low, 0.0, far)), axis=0)
                for start in (0, half_rows):
                    at_row = start + (2 * column + parity) * 2 * length
                    values[slot, c // per_group, at_row : at_row + 2 * length, :] = pair.astype(BF16)

    def write(index):
        row = places[index]
        served = index < places[store_rows]
        slot = jnp.bitwise_xor(order[jnp.minimum(index, devices - 1)], me[0])
        for g in range(groups):
            product = lax.dot_general(
                keys[slot, g], values[slot, g], (((0,), (0,)), ((), ())), preferred_element_type=F32
            )
            for head in range(8):
                for tile in range(0, tiles, 8):
                    at = head * tiles + tile
                    turned[index % 2, g, pl.ds(head + 8 * tile, 8, stride=8), :] = product[at : at + 8]
            for tile in range(tiles):
                at = slice(tile * LANES, (tile + 1) * LANES)
                added = jnp.where(served, turned[index % 2, g, tile * 8 : tile * 8 + 8, :], 0.0)
                result[row, g * 8 : g * 8 + 8, at] = scaled[row, g * 8 : g * 8 + 8, at] + added
        flush(row).start()

    def flush(row):
        return pltpu.make_async_copy(result.at[row], out.at[row], sems.at[row])

    loop(store_rows, write)
    loop(store_rows, lambda row: flush(row).wait())


def local_kernel(r, k, v, w, bonus, after, out):
    del after
    length = 8
    sessions = r.shape[0] // length
    columns = r.shape[1] // LANES
    low = lane_ids(length) < GROUP_WIDTH
    rows = row_ids(length)

    @pl.loop(0, sessions)
    def _(j):
        at = pl.ds(pl.multiple_of(j * length, length), length)
        for c in range(columns):
            cols = slice(c * LANES, (c + 1) * LANES)
            step, total = running_decay(w[at, cols])
            query = r[at, cols].astype(F32)
            key = k[at, cols].astype(F32)
            value = v[at, cols].astype(F32)
            wkv = half_sums(query * bonus[:, cols] * key, low) * value
            decayed = query * jnp.exp(total - step)
            grown = key * jnp.exp(-total)
            for back in range(1, length):
                score = half_sums(decayed * pltpu.roll(grown, back, 0), low)
                wkv = wkv + jnp.where(rows >= back, score * pltpu.roll(value, back, 0), 0.0)
            out[at, cols] = wkv


def finish_kernel(route, recv, part, gate, gain, shift, out):
    _, length, channels = recv.shape
    low = lane_ids(length) < GROUP_WIDTH
    rows = row_ids(length)
    for j in range(out.shape[0] // length):
        owner, count = route[2 * j], route[2 * j + 1]
        at = slice(j * length, (j + 1) * length)
        for c in range(channels // LANES):
            cols = slice(c * LANES, (c + 1) * LANES)
            wkv = recv[owner, :, cols] + part[at, cols]
            centred = wkv - half_sums(wkv, low) * (1.0 / GROUP_WIDTH)
            variance = half_sums(centred * centred, low) * (1.0 / GROUP_WIDTH)
            normed = centred * lax.rsqrt(variance + EPS) * gain[:, cols] + shift[:, cols]
            g = gate[at, cols].astype(F32)
            gated = normed * (g / (1.0 + jnp.exp(-g)))
            out[at, cols] = jnp.where(rows < count, gated, 0.0).astype(BF16)


def cost(flops, nbytes):
    return pl.CostEstimate(flops=flops, bytes_accessed=nbytes, transcendentals=0)


PARAMS = pltpu.CompilerParams(vmem_limit_bytes=24 * 2**20)


def in_vmem(x):
    return pltpu.with_memory_space_constraint(x, pltpu.VMEM)


def in_hbm(x):
    return pltpu.with_memory_space_constraint(x, pltpu.HBM)


def in_smem(x):
    return pltpu.with_memory_space_constraint(x, pltpu.SMEM)


def step(r, k, v, w, gate, bonus, gain, shift, store, hold, label, count):
    devices = lax.axis_size("cache")
    sessions = label.shape[0]
    store_rows, heads, state = store.shape
    tokens, channels = r.shape
    length = tokens // sessions
    me = lax.axis_index("cache").astype(jnp.int32).reshape(1)
    hbm = pl.BlockSpec(memory_space=pltpu.HBM)
    anywhere = pl.BlockSpec(memory_space=pl.ANY)
    send, slots, route = pl.pallas_call(
        functools.partial(pack_kernel, store_rows),
        out_shape=(
            jax.ShapeDtypeStruct((devices, length, 2 * channels + META), BF16),
            jax.ShapeDtypeStruct((devices, length, 2 * channels), BF16),
            pltpu.SMEM((2 * sessions,), jnp.int32),
        ),
        in_specs=[SMEM()] + [hbm] * 7,
        out_specs=(hbm, anywhere, SMEM()),
        scratch_shapes=[
            pltpu.SMEM(hold.shape, jnp.int32),
            pltpu.SMEM(label.shape, jnp.int32),
            pltpu.SMEM(count.shape, jnp.int32),
            pltpu.VMEM((devices, length, META), BF16),
            pltpu.VMEM((4, tokens, channels), BF16),
            pltpu.SemaphoreType.DMA((7,)),
            pltpu.SemaphoreType.DMA((4 * sessions + 1,)),
        ],
        compiler_params=PARAMS,
        name="pack",
    )(me, *(in_hbm(x) for x in (hold, label, count, r, w, k, v)))
    recv = in_vmem(lax.all_to_all(send, "cache", split_axis=0, concat_axis=0, tiled=True))

    half = devices // 2
    arrays = [slots]
    where = {0: (0, 0)}
    for step in range(1, half):
        pair = slots[2 * step : 2 * step + 2]
        arrays.append(lax.ppermute(pair, "cache", [(i, i ^ step) for i in range(devices)]))
        where[step] = (step, 0)
    groups, depth = heads // 8, 8 * state // LANES
    matrices, resident = pl.pallas_call(
        retile_kernel,
        out_shape=(
            pltpu.VMEM((store_rows, groups, depth, 2 * LANES), BF16),
            pltpu.VMEM(store.shape, F32),
        ),
        in_specs=[VMEM(), hbm],
        out_specs=(VMEM(), VMEM()),
        scratch_shapes=[pltpu.VMEM((groups, depth, LANES), F32)],
        cost_estimate=cost(8_000_000, 2_000_000),
        compiler_params=PARAMS,
        name="retile",
    )(in_hbm(store), send)
    back, table, order, places = pl.pallas_call(
        state_read_kernel,
        out_shape=(
            jax.ShapeDtypeStruct((devices, length, channels), F32),
            pltpu.SMEM((devices,), jnp.int32),
            pltpu.SMEM((devices,), jnp.int32),
            pltpu.SMEM((store_rows + 1,), jnp.int32),
        ),
        in_specs=[VMEM()] * 2,
        out_specs=(hbm, SMEM(), SMEM(), SMEM()),
        scratch_shapes=[
            pltpu.VMEM((devices, groups, 4 * 8 * length, depth), BF16),
            pltpu.VMEM((min(devices, store_rows), length, channels), F32),
            pltpu.SMEM((store_rows,), jnp.int32),
            pltpu.SemaphoreType.DMA((min(devices, store_rows),)),
        ],
        compiler_params=PARAMS,
        name="state_read",
    )(recv, in_vmem(matrices))
    relay = pl.pallas_call(
        collect_kernel,
        out_shape=pltpu.VMEM((half, length, 2 * channels), BF16),
        in_specs=[anywhere] * (half + 1),
        out_specs=VMEM(),
        scratch_shapes=[pltpu.SemaphoreType.DMA((half,))],
        compiler_params=PARAMS,
        name="collect",
    )(back, *arrays)
    arrays.append(lax.ppermute(relay, "cache", [(i, i ^ half) for i in range(devices)]))
    for step in range(half):
        where[half + step] = (half, step)

    table, order, places = in_smem(table), in_smem(order), in_smem(places)
    returned = in_vmem(lax.all_to_all(back, "cache", split_axis=0, concat_axis=0, tiled=True))
    part = pl.pallas_call(
        local_kernel,
        out_shape=pltpu.VMEM((tokens, channels), F32),
        in_specs=[VMEM()] * 5 + [hbm],
        out_specs=VMEM(),
        cost_estimate=cost(8_000_000, 400_000),
        compiler_params=PARAMS,
        name="local",
    )(*(in_hbm(x) for x in (r, k, v, w, bonus.reshape(1, channels))), send)
    scaled, gaps = pl.pallas_call(
        scale_kernel,
        out_shape=(
            pltpu.VMEM(store.shape, F32),
            pltpu.VMEM((devices, length, channels), F32),
        ),
        in_specs=[SMEM()] * 3 + [VMEM()] * 2 + [hbm],
        out_specs=(VMEM(), VMEM()),
        scratch_shapes=[pltpu.VMEM((heads * length, LANES), F32)],
        cost_estimate=cost(8_000_000, 400_000),
        compiler_params=PARAMS,
        name="scale",
    )(table, order, places, recv, in_vmem(resident), back)
    updated = pl.pallas_call(
        functools.partial(state_write_kernel, [where[slot] for slot in range(devices)]),
        out_shape=jax.ShapeDtypeStruct(store.shape, F32),
        in_specs=[SMEM()] * 3 + [VMEM()] * (2 + len(arrays)),
        out_specs=hbm,
        scratch_shapes=[
            pltpu.VMEM((devices, groups, 4 * 8 * length, depth), BF16),
            pltpu.VMEM((devices, groups, 4 * 8 * length, LANES), BF16),
            pltpu.VMEM((2, groups, depth, LANES), F32),
            pltpu.VMEM(store.shape, F32),
            pltpu.SemaphoreType.DMA((store_rows,)),
        ],
        cost_estimate=cost(8_000_000, 3_000_000),
        compiler_params=PARAMS,
        name="state_write",
    )(order, places, me, in_vmem(gaps), in_vmem(scaled), *(in_vmem(x) for x in arrays))
    mixed = pl.pallas_call(
        finish_kernel,
        out_shape=jax.ShapeDtypeStruct((tokens, channels), BF16),
        in_specs=[SMEM()] + [VMEM()] * 5,
        out_specs=VMEM(),
        compiler_params=PARAMS,
        name="finish",
    )(
        in_smem(route),
        returned,
        in_vmem(part),
        in_vmem(gate),
        gain.reshape(1, channels),
        shift.reshape(1, channels),
    )
    return mixed, updated


def solution(mesh):
    rows = P(("groups", "cache"), "mp")
    states = P(("groups", "cache"), "mp", None)
    owned = P(("groups", "cache"))
    in_specs = (rows,) * 5 + (P("mp"),) * 3 + (states, P("groups"), owned, owned)
    return jax.shard_map(
        step, mesh=mesh, in_specs=in_specs, out_specs=(rows, states), check_vma=False
    )
```
